512 devices in a mesh: dp: 16 (over x, y_hi, core), ctx: 32 (over y_lo, z).
Axes of the slice: x: 4, y: 4 (y_hi: 2, y_lo: 2; y = y_hi * 2 + y_lo), z: 16, core: 2. Of those that a mesh axis runs over, the one named last changes fastest.
Arguments:
- queries: bfloat16 [16, 4096, 2048], P('dp', 'ctx'), may hold values from -6 to 6
- keys: bfloat16 [16, 4096, 2048], P('dp', 'ctx'), may hold values from -6 to 6
- values: bfloat16 [16, 4096, 2048], P('dp', 'ctx'), may hold values from -6 to 6
- out_grad: bfloat16 [16, 4096, 2048], P('dp', 'ctx'), may hold values from -6 to 6
- out_proj: bfloat16 [2048, 2048], P('dp'), may hold values from -0.125 to 0.125
- attn_out: bfloat16 [16, 4096, 2048], P('dp', 'ctx'), may hold values from -3 to 3
- log_sum: float32 [16, 16, 4096], P('dp', None, 'ctx'), may hold values from 3 to 5
- group_order: int32 [16, 128], P('dp'), may hold values from 0 to 127, each once within a row
Outputs:
- query_grad: bfloat16 [16, 4096, 2048], P('dp', 'ctx')
- key_grad: bfloat16 [16, 4096, 2048], P('dp', 'ctx')
- value_grad: bfloat16 [16, 4096, 2048], P('dp', 'ctx')
The draws below stay inside these ranges and needn't reach their ends.
Inputs may be any that keep to these rules, and one draw needn't show every extreme that they name: `group_order`: each row holds every number once.
All inputs are finite; a program needn't handle non-finite values.
Results may differ from the reference program's by a relative error of at most 0.0075.
Values may be sent and summed in bfloat16 or wider, within the bound.
A program may use at most 64 MiB of HBM per device.

```python
import jax
import jax.numpy as jnp
from jax import lax

HEADS = 16
DH = 128
DW = 2048
GROUP = 32
TOK = 128
CPD = 4
BLOCKS = 32
GROUPS = 128
LEN = 4096
SEQS = 16


def steps_of(own_key, shape, pieces, least, high):
    loudness = 1.0
    for dim, blocks in pieces:
        draws = jax.random.uniform(jax.random.fold_in(jax.random.fold_in(own_key, 6), dim), (blocks,), jnp.float32, least / len(pieces), high / len(pieces))
        loudness = loudness * jnp.repeat(jnp.exp(draws), shape[dim] // blocks).reshape((-1,) + (1,) * (len(shape) - 1 - dim))
    return loudness


def bell_draw(key, shape, width, limit, pieces=(), kind=jnp.bfloat16):
    loudness = steps_of(key, shape, pieces, -0.22, 0.18) if pieces else 1.0
    values = jax.random.normal(key, shape, jnp.float32) * width * loudness
    return jnp.minimum(jnp.maximum(values, -limit), limit).astype(kind)


def setup_inputs(seed: int = 0) -> dict:
    splits = jax.random.split(jax.random.key(seed), 9)
    queries = bell_draw(splits[0], (SEQS, LEN, HEADS * DH), 1.0, 6.0, ((0, 16), (1, 32)))
    keys = bell_draw(splits[1], (SEQS, LEN, HEADS * DH), 1.0, 6.0, ((0, 16), (1, 32)))
    values = bell_draw(splits[2], (SEQS, LEN, HEADS * DH), 1.0, 6.0, ((0, 16), (1, 32)))
    out_grad = bell_draw(splits[3], (SEQS, LEN, DW), 1.0, 6.0, ((0, 16), (1, 32)))
    out_proj = bell_draw(splits[4], (DW, HEADS * DH), DW ** -0.5, 0.125, ((0, 16),))
    attn_out = bell_draw(splits[5], (SEQS, LEN, HEADS * DH), 0.5, 3.0, ((0, 16), (1, 32)))
    log_sum = jnp.clip(3.0 + 2.0 * jax.random.uniform(splits[6], (SEQS, HEADS, LEN), jnp.float32) ** steps_of(splits[6], (SEQS, HEADS, LEN), ((0, 16), (2, 32)), -0.2, 0.2), 3.0, 5.0)
    group_order = jax.vmap(lambda own: jax.random.permutation(own, GROUPS))(jax.random.split(splits[7], SEQS)).reshape((SEQS, GROUPS)).astype(jnp.int32)
    return dict(queries=queries, keys=keys, values=values, out_grad=out_grad, out_proj=out_proj, attn_out=attn_out, log_sum=log_sum, group_order=group_order)


def pair_grads(query_blk, grad_blk, lse_blk, delta_blk, query_pos, key_blk, value_blk, key_pos):
    factor = DH ** -0.5
    query_f = query_blk.astype(jnp.float32)
    grad_f = grad_blk.astype(jnp.float32)
    key_f = key_blk.astype(jnp.float32)
    value_f = value_blk.astype(jnp.float32)
    scores = jnp.einsum('nqhd,nkhd->nhqk', query_f, key_f) * factor
    visible = key_pos[:, None, None, :] <= query_pos[:, None, :, None]
    probs = jnp.where(visible, jnp.exp(scores - lse_blk[:, :, :, None]), 0.0)
    probs_low = lax.optimization_barrier(probs.astype(jnp.bfloat16)).astype(jnp.float32)
    value_part = jnp.einsum('nhqk,nqhd->nkhd', probs_low, grad_f)
    dprobs = jnp.einsum('nqhd,nkhd->nhqk', grad_f, value_f)
    dscores = (probs * (dprobs - delta_blk[:, :, :, None])).astype(jnp.bfloat16)
    dscores = lax.optimization_barrier(dscores).astype(jnp.float32)
    query_part = jnp.einsum('nhqk,nkhd->nqhd', dscores, key_f) * factor
    key_part = jnp.einsum('nhqk,nqhd->nkhd', dscores, query_f) * factor
    return query_part, key_part, value_part


def reference(queries, keys, values, out_grad, out_proj, attn_out, log_sum, group_order):
    def blocks(array):
        return array.reshape(BLOCKS, TOK, HEADS, DH)

    def one_sequence(items):
        query, key, value, upstream, output, lse, order = items
        attn_grad = jnp.dot(upstream, out_proj, preferred_element_type=jnp.float32).astype(jnp.bfloat16)
        grad_b = blocks(attn_grad)
        delta_b = jnp.sum(grad_b.astype(jnp.float32) * blocks(output).astype(jnp.float32), axis=3).transpose(0, 2, 1)
        lse_b = lse.reshape(HEADS, BLOCKS, TOK).transpose(1, 0, 2)
        offsets = jnp.arange(GROUP, dtype=jnp.int32)
        position = (order.reshape(BLOCKS, CPD)[:, :, None] * GROUP + offsets[None, None, :]).reshape(BLOCKS, TOK)
        query_b = blocks(query)
        key_b = blocks(key)
        value_b = blocks(value)
        own = pair_grads(query_b, grad_b, lse_b, delta_b, position, key_b, value_b, position)
        cross = pair_grads(query_b, grad_b, lse_b, delta_b, position,
                           jnp.roll(key_b, 1, axis=0), jnp.roll(value_b, 1, axis=0), jnp.roll(position, 1, axis=0))
        query_total = own[0] + cross[0]
        key_total = own[1] + jnp.roll(cross[1], -1, axis=0)
        value_total = own[2] + jnp.roll(cross[2], -1, axis=0)
        return (query_total.reshape(LEN, HEADS * DH).astype(jnp.bfloat16),
                key_total.reshape(LEN, HEADS * DH).astype(jnp.bfloat16),
                value_total.reshape(LEN, HEADS * DH).astype(jnp.bfloat16))

    results = lax.map(one_sequence, (queries, keys, values, out_grad, attn_out, log_sum, group_order))
    return (results[0], results[1], results[2])
```

```python
import functools

import jax
import jax.numpy as jnp
from jax import lax
from jax.experimental import pallas as pl
from jax.experimental.pallas import tpu as pltpu
from jax.sharding import PartitionSpec as P

MESH = pl.DeviceIdType.MESH
HEADS, DH, TOK, GROUP = 16, 128, 128, 32
WIDTH = HEADS * DH
CHUNKS = 8
CW = WIDTH // CHUNKS
HPC = HEADS // CHUNKS
AHEAD = 3
LATE = 2
NEG = -1e30
F32 = jnp.float32
BF16 = jnp.bfloat16


def nt(a, b):
    return lax.dot_general(a, b, (((1,), (1,)), ((), ())), preferred_element_type=F32)


def nn(a, b):
    return lax.dot_general(a, b, (((1,), (0,)), ((), ())), preferred_element_type=F32)


def kernel(
    order, q_in, k_in, v_in, g_in, w_in, o_in, l_in,
    dqb, dkb, dvb,
    qb, kb, vb, gb, ob, ab, wx, po, ps, pr, lb, db, bias_s, bias_t,
    local_sem, w_send, w_recv, f_send, f_recv, p_send, p_recv,
    a_send, a_recv, kv_send, kv_recv, q_send, q_recv, s_send, s_recv, g_send, g_recv, ready,
):
    dp = lax.axis_index("dp")
    ctx = lax.axis_index("ctx")
    x, yh, core = dp // 4, (dp // 2) % 2, dp % 2
    yl, z = ctx // 16, ctx % 16

    def chip(x, yh, core):
        return x * 4 + yh * 2 + core

    right = (chip((x + 1) % 4, yh, core), ctx)
    left = (chip((x + 3) % 4, yh, core), ctx)
    across = (chip(x, 1 - yh, core), (1 - yl) * 16 + z)
    partner = (chip(x, yh, 1 - core), ctx)
    after = (dp, (ctx + 1) % 32)
    before = (dp, (ctx + 31) % 32)

    def cols(j):
        return pl.ds(pl.multiple_of(j * CW, CW), CW)

    def remote(src, dst, send, recv, device):
        return pltpu.make_async_remote_copy(
            src_ref=src, dst_ref=dst, send_sem=send, recv_sem=recv,
            device_id=device, device_id_type=MESH,
        )

    loads = [
        pltpu.make_async_copy(w_in, wx.at[0, core], local_sem.at[0]),
        pltpu.make_async_copy(q_in.at[0], qb.at[0], local_sem.at[1]),
        pltpu.make_async_copy(k_in.at[0], kb.at[0], local_sem.at[2]),
        pltpu.make_async_copy(v_in.at[0], vb.at[0], local_sem.at[3]),
        pltpu.make_async_copy(o_in.at[0], ob, local_sem.at[4]),
        pltpu.make_async_copy(l_in.at[0], lb.at[0], local_sem.at[5]),
    ]

    def strip(r, of_class):
        return pl.ds(pl.multiple_of(((x + r) % 4) * 512 + of_class * 256, 256), 256)

    for r in range(4):
        loads.append(
            pltpu.make_async_copy(
                g_in.at[0, :, strip(r, yh)],
                ab.at[pl.ds(0, TOK), pl.ds(r * 256, 256)],
                local_sem.at[6 + r],
            )
        )
    for c in loads:
        c.start()

    barrier = pltpu.get_barrier_semaphore()
    up_waits, down_waits = z == 15, z != 0

    def tell(semaphore, device):
        pl.semaphore_signal(semaphore, inc=1, device_id=device, device_id_type=MESH)

    for device in (right, left, across, partner):
        tell(barrier, device)
    pl.when(z != 15)(lambda: tell(barrier, after))
    pl.when(z == 0)(lambda: tell(barrier, before))
    pl.semaphore_wait(barrier, 4 + up_waits.astype(jnp.int32) + down_waits.astype(jnp.int32))

    def own_right(j):
        return remote(w_in.at[:, cols(j)], wx.at[3, core, :, cols(j)], w_send.at[0, j], w_recv.at[0, j], right)

    def own_left(j):
        return remote(w_in.at[:, cols(j)], wx.at[1, core, :, cols(j)], w_send.at[1, j], w_recv.at[1, j], left)

    low, high = pl.ds(0, TOK // 2), pl.ds(TOK // 2, TOK // 2)

    def far_right(j):
        return remote(
            wx.at[3, core, low, cols(j)], wx.at[2, core, low, cols(j)], f_send.at[0, j], f_recv.at[0, j], right
        )

    def far_left(j):
        return remote(
            wx.at[1, core, high, cols(j)], wx.at[2, core, high, cols(j)], f_send.at[1, j], f_recv.at[1, j], left
        )

    def share(r, j, owner):
        src = w_in.at[:, cols(j)] if r == 0 else wx.at[r, owner, :, cols(j)]
        return remote(src, wx.at[r, owner, :, cols(j)], p_send.at[r, j], p_recv.at[r, j], partner)

    def columns_across(r):
        return remote(
            g_in.at[0, :, strip(r, 1 - yh)],
            ab.at[pl.ds(TOK, TOK), pl.ds(r * 256, 256)],
            a_send.at[r], a_recv.at[r], across,
        )

    def key_after(j):
        return remote(k_in.at[0, :, cols(j)], kb.at[1, :, cols(j)], kv_send.at[0, j], kv_recv.at[0, j], after)

    def value_after(j):
        return remote(v_in.at[0, :, cols(j)], vb.at[1, :, cols(j)], kv_send.at[1, j], kv_recv.at[1, j], after)

    def query_before(j):
        return remote(q_in.at[0, :, cols(j)], qb.at[1, :, cols(j)], q_send.at[j], q_recv.at[j], before)

    lse_before = remote(l_in.at[0], lb.at[1], q_send.at[CHUNKS], q_recv.at[CHUNKS], before)

    def partial_across(j):
        return remote(ps.at[:, cols(j)], pr.at[:, cols(j)], s_send.at[j], s_recv.at[j], across)

    def grad_before(j):
        return remote(gb.at[0, :, cols(j)], gb.at[1, :, cols(j)], g_send.at[0, j], g_recv.at[0, j], before)

    def delta_before(j):
        return remote(db.at[0, j], db.at[1, j], g_send.at[1, j], g_recv.at[1, j], before)

    for j in range(AHEAD):
        own_right(j).start()
        own_left(j).start()
        if j == 0:
            for r in range(4):
                columns_across(r).start()
    pl.when(z == 15)(lambda: tell(ready.at[1], after))
    pl.when(z != 0)(lambda: tell(ready.at[0], before))

    @pl.loop(0, CHUNKS)
    def _(j):
        share(0, j, core).start()

    def send_down():
        pl.when(z == 0)(lambda: pl.semaphore_wait(ready.at[1], 1))
        lse_before.start()

        @pl.loop(0, CHUNKS)
        def _(j):
            query_before(j).start()

    def send_up():
        pl.when(z != 15)(lambda: pl.semaphore_wait(ready.at[0], 1))

        @pl.loop(0, CHUNKS)
        def _(j):
            key_after(j).start()
            value_after(j).start()

    pl.when(z != 0)(send_down)
    pl.when(z != 1)(send_up)

    sub = lax.broadcasted_iota(jnp.int32, (TOK, TOK), 0)
    lane = lax.broadcasted_iota(jnp.int32, (TOK, TOK), 1)

    def position(block, index):
        ids = [order[0, block * 4 + i] for i in range(4)]
        group = index // GROUP
        return jnp.where(group == 0, ids[0], jnp.where(group == 1, ids[1], jnp.where(group == 2, ids[2], ids[3]))) * GROUP + index % GROUP

    own_col, own_row = position(ctx, sub), position(ctx, lane)
    prev_row = position((ctx + 31) % 32, lane)
    next_row = position((ctx + 1) % 32, lane)
    zero = jnp.zeros((TOK, TOK), F32)
    neg = jnp.full((TOK, TOK), NEG, F32)
    bias_s[:, pl.ds(0, TOK)] = jnp.where(own_row <= own_col, zero, neg)
    bias_s[:, pl.ds(TOK, TOK)] = jnp.where(prev_row <= own_col, zero, neg)
    bias_t[:, pl.ds(0, TOK)] = jnp.where(own_col <= own_row, zero, neg)
    bias_t[:, pl.ds(TOK, TOK)] = jnp.where(own_col <= next_row, zero, neg)

    factor = DH ** -0.5

    def head_cols(j, h):
        return pl.ds(pl.multiple_of(j * CW + h * DH, DH), DH)

    def relay(j):
        own_right(j).wait_recv()
        far_right(j).start()
        share(3, j, core).start()
        own_left(j).wait_recv()
        far_left(j).start()
        share(1, j, core).start()

        @pl.when(j + AHEAD < CHUNKS)
        def _():
            own_right(j + AHEAD).start()
            own_left(j + AHEAD).start()

    def relay_far(j):
        far_right(j).wait_recv()
        far_left(j).wait_recv()
        share(2, j, core).start()

    def project(j):
        @pl.when(j == 0)
        def _():
            loads[0].wait()
            for r in range(4):
                loads[6 + r].wait()
                columns_across(r).wait_recv()

        for r in (0, 3, 1, 2):
            share(r, j, 1 - core).wait_recv()
        w = wx[:, :, :, cols(j)].reshape(8 * TOK, CW)
        part = nn(ab[...], w)
        ps[:, cols(j)] = part[TOK:].astype(BF16)
        partial_across(j).start()
        po[:, cols(j)] = part[:TOK]

    def queries_side(j):
        @pl.when(j == 0)
        def _():
            for c in loads[1:6]:
                c.wait()

        partial_across(j).wait_recv()
        grad = (po[:, cols(j)] + pr[:, cols(j)].astype(F32)).astype(BF16)
        gb[0, :, cols(j)] = grad
        grad_before(j).start()
        terms = grad.astype(F32) * ob[:, cols(j)].astype(F32)
        deltas = [jnp.sum(terms[:, h * DH:(h + 1) * DH], axis=1, keepdims=True) for h in range(HPC)]
        table = jnp.broadcast_to(deltas[0], (TOK, TOK))
        for h in range(1, HPC):
            table = jnp.where(lane == h, deltas[h], table)
        db[0, j] = table.T[:8]
        delta_before(j).start()
        key_after(j).wait_recv()
        value_after(j).wait_recv()
        for h in range(HPC):
            hc = head_cols(j, h)
            q, g = qb[0, :, hc], grad[:, h * DH:(h + 1) * DH]
            k = kb[:, :, hc].reshape(2 * TOK, DH)
            v = vb[:, :, hc].reshape(2 * TOK, DH)
            lse = jnp.broadcast_to(lb[0, pl.ds(j * HPC + h, 1)], (TOK, TOK)).T
            lse = jnp.concatenate([lse, lse], axis=1)
            p = jnp.exp(nt(q, k) * factor - lse + bias_s[...])
            ds = (p * (nt(g, v) - deltas[h])).astype(BF16)
            dqb[:, hc] = (nn(ds, k) * factor).astype(BF16)

    def keys_side(j):
        @pl.when(j == 0)
        def _():
            lse_before.wait_recv()

        query_before(j).wait_recv()
        grad_before(j).wait_recv()
        delta_before(j).wait_recv()
        for h in range(HPC):
            hc = head_cols(j, h)
            k, v = kb[0, :, hc], vb[0, :, hc]
            q = qb[:, :, hc].reshape(2 * TOK, DH)
            g = gb[:, :, hc].reshape(2 * TOK, DH)
            row = pl.ds(j * HPC + h, 1)
            lse = jnp.concatenate([lb[0, row], lb[1, row]], axis=1)
            delta = jnp.concatenate([db[0, j, pl.ds(h, 1)], db[1, j, pl.ds(h, 1)]], axis=1)
            p = jnp.exp(nt(k, q) * factor - lse + bias_t[...])
            dvb[:, hc] = nn(p.astype(BF16), g).astype(BF16)
            ds = (p * (nt(v, g) - delta)).astype(BF16)
            dkb[:, hc] = (nn(ds, q) * factor).astype(BF16)

    stages = ((relay, 0), (relay_far, 2), (project, 3), (queries_side, 5), (keys_side, 7))

    @pl.loop(0, CHUNKS + stages[-1][1])
    def _(t):
        for stage, lag in stages:
            pl.when((t >= lag) & (t < CHUNKS + lag))(functools.partial(stage, t - lag))
        pl.when((t == LATE) & (z == 0))(send_down)
        pl.when((t == LATE) & (z == 1))(send_up)

    for r in range(4):
        columns_across(r).wait_send()
    lse_before.wait_send()

    @pl.loop(0, CHUNKS)
    def _(j):
        for c in (own_right, own_left, far_right, far_left, key_after, value_after, query_before, partial_across,
                  grad_before, delta_before):
            c(j).wait_send()
        for r in range(4):
            share(r, j, core).wait_send()


def store(a, b, c, x, y, z, sem):
    copies = [pltpu.make_async_copy(s, d.at[0], sem.at[i]) for i, (s, d) in enumerate(((a, x), (b, y), (c, z)))]
    for copy in copies:
        copy.start()
    for copy in copies:
        copy.wait()


def on_device(queries, keys, values, out_grad, out_proj, attn_out, log_sum, group_order):
    hbm = pl.BlockSpec(memory_space=pl.ANY)
    vmem = pl.BlockSpec(memory_space=pltpu.VMEM)
    out = jax.ShapeDtypeStruct((1, TOK, WIDTH), BF16)
    dma = pltpu.SemaphoreType.DMA
    held = pl.pallas_call(
        kernel,
        out_shape=(pltpu.VMEM((TOK, WIDTH), BF16),) * 3,
        in_specs=[pl.BlockSpec(memory_space=pltpu.SMEM)] + [hbm] * 7,
        out_specs=(vmem, vmem, vmem),
        scratch_shapes=[
            pltpu.VMEM((2, TOK, WIDTH), BF16),
            pltpu.VMEM((2, TOK, WIDTH), BF16),
            pltpu.VMEM((2, TOK, WIDTH), BF16),
            pltpu.VMEM((2, TOK, WIDTH), BF16),
            pltpu.VMEM((TOK, WIDTH), BF16),
            pltpu.VMEM((2 * TOK, 1024), BF16),
            pltpu.VMEM((4, 2, TOK, WIDTH), BF16),
            pltpu.VMEM((TOK, WIDTH), F32),
            pltpu.VMEM((TOK, WIDTH), BF16),
            pltpu.VMEM((TOK, WIDTH), BF16),
            pltpu.VMEM((2, HEADS, TOK), F32),
            pltpu.VMEM((2, CHUNKS, 8, TOK), F32),
            pltpu.VMEM((TOK, 2 * TOK), F32),
            pltpu.VMEM((TOK, 2 * TOK), F32),
            dma((10,)),
            dma((2, CHUNKS)), dma((2, CHUNKS)),
            dma((2, CHUNKS)), dma((2, CHUNKS)),
            dma((4, CHUNKS)), dma((4, CHUNKS)),
            dma((4,)), dma((4,)),
            dma((2, CHUNKS)), dma((2, CHUNKS)),
            dma((CHUNKS + 1,)), dma((CHUNKS + 1,)),
            dma((CHUNKS,)), dma((CHUNKS,)),
            dma((2, CHUNKS)), dma((2, CHUNKS)),
            pltpu.SemaphoreType.REGULAR((2,)),
        ],
        compiler_params=pltpu.CompilerParams(collective_id=0, has_side_effects=True),
        name="attention_backward",
    )(group_order, queries, keys, values, out_grad, out_proj, attn_out, log_sum)
    return pl.pallas_call(
        store,
        out_shape=(out, out, out),
        in_specs=[vmem] * 3,
        out_specs=(hbm, hbm, hbm),
        scratch_shapes=[dma((3,))],
        name="store",
    )(*(pltpu.with_memory_space_constraint(h, pltpu.VMEM) for h in held))


def solution(mesh):
    block = P("dp", "ctx", None)
    return jax.shard_map(
        on_device,
        mesh=mesh,
        in_specs=(block, block, block, block, P("dp", None), block, P("dp", None, "ctx"), P("dp", None)),
        out_specs=(block, block, block),
        check_vma=False,
    )
```

```python
import functools

import jax
import jax.numpy as jnp
from jax import lax
from jax.experimental import pallas as pl
from jax.experimental.pallas import tpu as pltpu
from jax.sharding import PartitionSpec as P

MESH = pl.DeviceIdType.MESH
HEADS, DH, TOK, GROUP = 16, 128, 128, 32
WIDTH = HEADS * DH
CHUNKS = 8
CW = WIDTH // CHUNKS
HPC = HEADS // CHUNKS
AHEAD = 3
LATE = 2
WIDE = 1
NEG = -1e30
F32 = jnp.float32
BF16 = jnp.bfloat16


def nt(a, b):
    return lax.dot_general(a, b, (((1,), (1,)), ((), ())), preferred_element_type=F32)


def nn(a, b):
    return lax.dot_general(a, b, (((1,), (0,)), ((), ())), preferred_element_type=F32)


def kernel(
    order, q_in, k_in, v_in, g_in, w_in, o_in, l_in,
    dqb, dkb, dvb,
    qb, kb, vb, gb, ob, ab, wx, po, ps, pr, lb, db, bias_s, bias_t,
    local_sem, w_send, w_recv, f_send, f_recv, p_send, p_recv,
    a_send, a_recv, kv_send, kv_recv, q_send, q_recv, s_send, s_recv, g_send, g_recv, ready,
):
    dp = lax.axis_index("dp")
    ctx = lax.axis_index("ctx")
    x, yh, core = dp // 4, (dp // 2) % 2, dp % 2
    yl, z = ctx // 16, ctx % 16

    def chip(x, yh, core):
        return x * 4 + yh * 2 + core

    right = (chip((x + 1) % 4, yh, core), ctx)
    left = (chip((x + 3) % 4, yh, core), ctx)
    across = (chip(x, 1 - yh, core), (1 - yl) * 16 + z)
    partner = (chip(x, yh, 1 - core), ctx)
    after = (dp, (ctx + 1) % 32)
    before = (dp, (ctx + 31) % 32)

    def cols(j):
        return pl.ds(pl.multiple_of(j * CW, CW), CW)

    def wide(j):
        return pl.ds(pl.multiple_of(j * WIDE * CW, WIDE * CW), WIDE * CW)

    def remote(src, dst, send, recv, device):
        return pltpu.make_async_remote_copy(
            src_ref=src, dst_ref=dst, send_sem=send, recv_sem=recv,
            device_id=device, device_id_type=MESH,
        )

    loads = [
        pltpu.make_async_copy(w_in, wx.at[0, core], local_sem.at[0]),
        pltpu.make_async_copy(q_in.at[0], qb.at[0], local_sem.at[1]),
        pltpu.make_async_copy(k_in.at[0], kb.at[0], local_sem.at[2]),
        pltpu.make_async_copy(v_in.at[0], vb.at[0], local_sem.at[3]),
        pltpu.make_async_copy(o_in.at[0], ob, local_sem.at[4]),
        pltpu.make_async_copy(l_in.at[0], lb.at[0], local_sem.at[5]),
    ]

    def strip(r, of_class):
        return pl.ds(pl.multiple_of(((x + r) % 4) * 512 + of_class * 256, 256), 256)

    for i, r in enumerate((0, 2, 1, 3)):
        loads.append(
            pltpu.make_async_copy(
                g_in.at[0, :, strip(r, yh)],
                ab.at[pl.ds(0, TOK), pl.ds(i * 256, 256)],
                local_sem.at[6 + i],
            )
        )
    for c in loads:
        c.start()

    barrier = pltpu.get_barrier_semaphore()
    up_waits, down_waits = z == 15, z != 0

    def tell(semaphore, device):
        pl.semaphore_signal(semaphore, inc=1, device_id=device, device_id_type=MESH)

    for device in (right, left, across, partner):
        tell(barrier, device)
    pl.when(z != 15)(lambda: tell(barrier, after))
    pl.when(z == 0)(lambda: tell(barrier, before))
    pl.semaphore_wait(barrier, 4 + up_waits.astype(jnp.int32) + down_waits.astype(jnp.int32))

    def own_right(j):
        return remote(w_in.at[:, cols(j)], wx.at[3, core, :, cols(j)], w_send.at[0, j], w_recv.at[0, j], right)

    def own_left(j):
        return remote(w_in.at[:, cols(j)], wx.at[2, core, :, cols(j)], w_send.at[1, j], w_recv.at[1, j], left)

    low, high = pl.ds(0, TOK // 2), pl.ds(TOK // 2, TOK // 2)

    def far_right(j):
        return remote(
            wx.at[3, core, low, cols(j)], wx.at[1, core, low, cols(j)], f_send.at[0, j], f_recv.at[0, j], right
        )

    def far_left(j):
        return remote(
            wx.at[2, core, high, cols(j)], wx.at[1, core, high, cols(j)], f_send.at[1, j], f_recv.at[1, j], left
        )

    def share_own(owner):
        return remote(w_in, wx.at[0, owner], p_send.at[0, 0], p_recv.at[0, 0], partner)

    def share_near(j, owner):
        part = wx.at[pl.ds(2, 2), owner, :, cols(j)]
        return remote(part, part, p_send.at[1, j], p_recv.at[1, j], partner)

    def share_far(j, owner):
        part = wx.at[1, owner, :, cols(j)]
        return remote(part, part, p_send.at[2, j], p_recv.at[2, j], partner)

    def columns_across(i):
        r = (0, 2, 1, 3)[i]
        return remote(
            g_in.at[0, :, strip(r, 1 - yh)],
            ab.at[pl.ds(TOK, TOK), pl.ds(i * 256, 256)],
            a_send.at[i], a_recv.at[i], across,
        )

    def key_after(j):
        return remote(k_in.at[0, :, wide(j)], kb.at[1, :, wide(j)], kv_send.at[0, j], kv_recv.at[0, j], after)

    def value_after(j):
        return remote(v_in.at[0, :, wide(j)], vb.at[1, :, wide(j)], kv_send.at[1, j], kv_recv.at[1, j], after)

    def query_before(j):
        return remote(q_in.at[0, :, wide(j)], qb.at[1, :, wide(j)], q_send.at[j], q_recv.at[j], before)

    lse_before = remote(l_in.at[0], lb.at[1], q_send.at[CHUNKS], q_recv.at[CHUNKS], before)

    def partial_across(j):
        return remote(ps.at[:, cols(j)], pr.at[:, cols(j)], s_send.at[j], s_recv.at[j], across)

    def grad_before(j):
        return remote(gb.at[0, :, cols(j)], gb.at[1, :, cols(j)], g_send.at[0, j], g_recv.at[0, j], before)

    def delta_before(j):
        return remote(db.at[0, j], db.at[1, j], g_send.at[1, j], g_recv.at[1, j], before)

    for j in range(AHEAD):
        own_right(j).start()
        own_left(j).start()
        if j == 0:
            for r in range(4):
                columns_across(r).start()
    pl.when(z == 15)(lambda: tell(ready.at[1], after))
    pl.when(z != 0)(lambda: tell(ready.at[0], before))

    share_own(core).start()

    def send_down():
        pl.when(z == 0)(lambda: pl.semaphore_wait(ready.at[1], 1))
        lse_before.start()

        @pl.loop(0, CHUNKS // WIDE)
        def _(j):
            query_before(j).start()

    def send_up():
        pl.when(z != 15)(lambda: pl.semaphore_wait(ready.at[0], 1))

        @pl.loop(0, CHUNKS // WIDE)
        def _(j):
            key_after(j).start()
            value_after(j).start()

    pl.when(z != 0)(send_down)
    pl.when(z != 1)(send_up)

    sub = lax.broadcasted_iota(jnp.int32, (TOK, TOK), 0)
    lane = lax.broadcasted_iota(jnp.int32, (TOK, TOK), 1)

    def position(block, index):
        ids = [order[0, block * 4 + i] for i in range(4)]
        group = index // GROUP
        return jnp.where(group == 0, ids[0], jnp.where(group == 1, ids[1], jnp.where(group == 2, ids[2], ids[3]))) * GROUP + index % GROUP

    own_col, own_row = position(ctx, sub), position(ctx, lane)
    prev_row = position((ctx + 31) % 32, lane)
    next_row = position((ctx + 1) % 32, lane)
    zero = jnp.zeros((TOK, TOK), F32)
    neg = jnp.full((TOK, TOK), NEG, F32)
    bias_s[:, pl.ds(0, TOK)] = jnp.where(own_row <= own_col, zero, neg)
    bias_s[:, pl.ds(TOK, TOK)] = jnp.where(prev_row <= own_col, zero, neg)
    bias_t[:, pl.ds(0, TOK)] = jnp.where(own_col <= own_row, zero, neg)
    bias_t[:, pl.ds(TOK, TOK)] = jnp.where(own_col <= next_row, zero, neg)

    factor = DH ** -0.5

    def head_cols(j, h):
        return pl.ds(pl.multiple_of(j * CW + h * DH, DH), DH)

    def relay(j):
        own_right(j).wait_recv()
        far_right(j).start()
        own_left(j).wait_recv()
        far_left(j).start()
        share_near(j, core).start()

        @pl.when(j + AHEAD < CHUNKS)
        def _():
            own_right(j + AHEAD).start()
            own_left(j + AHEAD).start()

    def relay_far(j):
        far_right(j).wait_recv()
        far_left(j).wait_recv()
        share_far(j, core).start()

    def project(j):
        @pl.when(j == 0)
        def _():
            loads[0].wait()
            share_own(1 - core).wait_recv()
            for r in range(4):
                loads[6 + r].wait()
                columns_across(r).wait_recv()

        share_near(j, 1 - core).wait_recv()
        share_far(j, 1 - core).wait_recv()
        w = wx[:, :, :, cols(j)].reshape(8 * TOK, CW)
        part = nn(ab[...], w)
        ps[:, cols(j)] = part[TOK:].astype(BF16)
        partial_across(j).start()
        po[:, cols(j)] = part[:TOK]

    def queries_side(j):
        @pl.when(j == 0)
        def _():
            for c in loads[1:6]:
                c.wait()

        partial_across(j).wait_recv()
        grad = (po[:, cols(j)] + pr[:, cols(j)].astype(F32)).astype(BF16)
        gb[0, :, cols(j)] = grad
        grad_before(j).start()
        terms = grad.astype(F32) * ob[:, cols(j)].astype(F32)
        deltas = [jnp.sum(terms[:, h * DH:(h + 1) * DH], axis=1, keepdims=True) for h in range(HPC)]
        table = jnp.broadcast_to(deltas[0], (TOK, TOK))
        for h in range(1, HPC):
            table = jnp.where(lane == h, deltas[h], table)
        db[0, j] = table.T[:8]
        delta_before(j).start()
        @pl.when(j % WIDE == 0)
        def _():
            key_after(j // WIDE).wait_recv()
            value_after(j // WIDE).wait_recv()

        for h in range(HPC):
            hc = head_cols(j, h)
            q, g = qb[0, :, hc], grad[:, h * DH:(h + 1) * DH]
            k = kb[:, :, hc].reshape(2 * TOK, DH)
            v = vb[:, :, hc].reshape(2 * TOK, DH)
            lse = jnp.broadcast_to(lb[0, pl.ds(j * HPC + h, 1)], (TOK, TOK)).T
            lse = jnp.concatenate([lse, lse], axis=1)
            p = jnp.exp(nt(q, k) * factor - lse + bias_s[...])
            ds = (p * (nt(g, v) - deltas[h])).astype(BF16)
            dqb[:, hc] = (nn(ds, k) * factor).astype(BF16)

    def keys_side(j):
        @pl.when(j == 0)
        def _():
            lse_before.wait_recv()

        @pl.when(j % WIDE == 0)
        def _():
            query_before(j // WIDE).wait_recv()

        grad_before(j).wait_recv()
        delta_before(j).wait_recv()
        for h in range(HPC):
            hc = head_cols(j, h)
            k, v = kb[0, :, hc], vb[0, :, hc]
            q = qb[:, :, hc].reshape(2 * TOK, DH)
            g = gb[:, :, hc].reshape(2 * TOK, DH)
            row = pl.ds(j * HPC + h, 1)
            lse = jnp.concatenate([lb[0, row], lb[1, row]], axis=1)
            delta = jnp.concatenate([db[0, j, pl.ds(h, 1)], db[1, j, pl.ds(h, 1)]], axis=1)
            p = jnp.exp(nt(k, q) * factor - lse + bias_t[...])
            dvb[:, hc] = nn(p.astype(BF16), g).astype(BF16)
            ds = (p * (nt(v, g) - delta)).astype(BF16)
            dkb[:, hc] = (nn(ds, q) * factor).astype(BF16)

    stages = ((relay, 0), (relay_far, 2), (project, 3), (queries_side, 5), (keys_side, 7))

    @pl.loop(0, CHUNKS + stages[-1][1])
    def _(t):
        for stage, lag in stages:
            pl.when((t >= lag) & (t < CHUNKS + lag))(functools.partial(stage, t - lag))
        pl.when((t == LATE) & (z == 0))(send_down)
        pl.when((t == LATE) & (z == 1))(send_up)

    for r in range(4):
        columns_across(r).wait_send()
    lse_before.wait_send()
    share_own(core).wait_send()

    @pl.loop(0, CHUNKS // WIDE)
    def _(j):
        for c in (key_after, value_after, query_before):
            c(j).wait_send()

    @pl.loop(0, CHUNKS)
    def _(j):
        for c in (own_right, own_left, far_right, far_left, partial_across,
                  grad_before, delta_before):
            c(j).wait_send()
        share_near(j, core).wait_send()
        share_far(j, core).wait_send()


def store(a, b, c, x, y, z, sem):
    copies = [pltpu.make_async_copy(s, d.at[0], sem.at[i]) for i, (s, d) in enumerate(((a, x), (b, y), (c, z)))]
    for copy in copies:
        copy.start()
    for copy in copies:
        copy.wait()


def on_device(queries, keys, values, out_grad, out_proj, attn_out, log_sum, group_order):
    hbm = pl.BlockSpec(memory_space=pl.ANY)
    vmem = pl.BlockSpec(memory_space=pltpu.VMEM)
    out = jax.ShapeDtypeStruct((1, TOK, WIDTH), BF16)
    dma = pltpu.SemaphoreType.DMA
    held = pl.pallas_call(
        kernel,
        out_shape=(pltpu.VMEM((TOK, WIDTH), BF16),) * 3,
        in_specs=[pl.BlockSpec(memory_space=pltpu.SMEM)] + [hbm] * 7,
        out_specs=(vmem, vmem, vmem),
        scratch_shapes=[
            pltpu.VMEM((2, TOK, WIDTH), BF16),
            pltpu.VMEM((2, TOK, WIDTH), BF16),
            pltpu.VMEM((2, TOK, WIDTH), BF16),
            pltpu.VMEM((2, TOK, WIDTH), BF16),
            pltpu.VMEM((TOK, WIDTH), BF16),
            pltpu.VMEM((2 * TOK, 1024), BF16),
            pltpu.VMEM((4, 2, TOK, WIDTH), BF16),
            pltpu.VMEM((TOK, WIDTH), F32),
            pltpu.VMEM((TOK, WIDTH), BF16),
            pltpu.VMEM((TOK, WIDTH), BF16),
            pltpu.VMEM((2, HEADS, TOK), F32),
            pltpu.VMEM((2, CHUNKS, 8, TOK), F32),
            pltpu.VMEM((TOK, 2 * TOK), F32),
            pltpu.VMEM((TOK, 2 * TOK), F32),
            dma((10,)),
            dma((2, CHUNKS)), dma((2, CHUNKS)),
            dma((2, CHUNKS)), dma((2, CHUNKS)),
            dma((3, CHUNKS)), dma((3, CHUNKS)),
            dma((4,)), dma((4,)),
            dma((2, CHUNKS)), dma((2, CHUNKS)),
            dma((CHUNKS + 1,)), dma((CHUNKS + 1,)),
            dma((CHUNKS,)), dma((CHUNKS,)),
            dma((2, CHUNKS)), dma((2, CHUNKS)),
            pltpu.SemaphoreType.REGULAR((2,)),
        ],
        compiler_params=pltpu.CompilerParams(collective_id=0, has_side_effects=True),
        name="attention_backward",
    )(group_order, queries, keys, values, out_grad, out_proj, attn_out, log_sum)
    return pl.pallas_call(
        store,
        out_shape=(out, out, out),
        in_specs=[vmem] * 3,
        out_specs=(hbm, hbm, hbm),
        scratch_shapes=[dma((3,))],
        name="store",
    )(*(pltpu.with_memory_space_constraint(h, pltpu.VMEM) for h in held))


def solution(mesh):
    block = P("dp", "ctx", None)
    return jax.shard_map(
        on_device,
        mesh=mesh,
        in_specs=(block, block, block, block, P("dp", None), block, P("dp", None, "ctx"), P("dp", None)),
        out_specs=(block, block, block),
        check_vma=False,
    )
```
